32 devices in a mesh: tm: 2 (over y), lon: 16 (over z, x, core).
Axes of the slice: x: 2, y: 2, z: 4, core: 2. Of those that a mesh axis runs over, the one named last changes fastest.
Arguments:
- first_guess: float32 [1, 8, 128, 128], P(None, 'tm', 'lon'), may hold values from -6 to 6
- observed: float32 [1, 8, 128, 128], P(None, 'tm', 'lon'), may hold values from -6 to 6
- obs_mask: int32 [1, 8, 128, 128], P(None, 'tm', 'lon'), may hold values 0 or 1
- land_mask: int32 [128, 128], P('lon'), may hold values 0 or 1
- enc_weight: float32 [32, 27], replicated, may hold values from -1.25 to 1.25
- enc_bias: float32 [32], replicated, may hold values from -0.5 to 0.5
- dec_weight: float32 [32, 27], replicated, may hold values from -0.21875 to 0.21875
- dec_bias: float32 [1], replicated, may hold values from -1 to 1
- gate_weight: bfloat16 [192, 441], replicated, may hold values from -0.25 to 0.25
- gate_bias: float32 [192], replicated, may hold values from -1 to 1
- out_weight: float32 [48], replicated, may hold values from -0.875 to 0.875
Outputs:
- analysis: float32 [1, 8, 128, 128], P(None, 'tm', 'lon')
The draws below stay inside these ranges and needn't reach their ends.
Inputs may be any that keep to these rules, and one draw needn't show every extreme that they name: `obs_mask`: 1 marks an observed cell on that day. `land_mask`: 1 marks a sea cell.
All inputs are finite; a program needn't handle non-finite values. No bound on the sum of `obs_mask` or of `land_mask` on one device may be relied on, other than what follows from the above.
Results may differ from the reference program's by a relative error of at most 0.00082.
Values may be sent and summed in bfloat16 or wider, within the bound.
A program may use at most 64 MiB of HBM per device.

```python
import jax
import jax.numpy as jnp
from jax import lax

SAMPLES = 1
LAT_CELLS = 128
PRIOR_CH = 32
STATE_CH = 48
SOLVER_ITERS = 2
GATE_CH = 192
WINDOW_DAYS = 8
LON_CELLS = 128


def set_ends(array, rng, low, high):
    shape = array.shape
    index_at = [jax.random.randint(jax.random.fold_in(rng, axis), (), 0, shape[axis]) for axis in range(len(shape))]
    array = array.at[tuple(index_at)].set(low)
    longest = shape.index(max(shape))
    index_at[longest] = (index_at[longest] + 1) % shape[longest]
    return array.at[tuple(index_at)].set(high)


def block_scale(stream_key, shape, split, least, largest):
    gain = 1.0
    for position, blocks in split:
        steps = jax.random.uniform(jax.random.fold_in(jax.random.fold_in(stream_key, 6), position), (blocks,), jnp.float32, least / len(split), largest / len(split))
        gain = gain * jnp.repeat(jnp.exp(steps), shape[position] // blocks).reshape((-1,) + (1,) * (len(shape) - 1 - position))
    return gain


def centred(key, dims, width, limit, shards=(), kind=jnp.bfloat16):
    drawn = width * jax.random.normal(key, dims, jnp.float32)
    if shards:
        drawn = drawn * block_scale(key, dims, shards, -0.22, 0.18)
    return jnp.clip(drawn, -limit, limit).astype(kind)


def setup_inputs(seed: int = 0) -> dict:
    arg_keys = jax.random.split(jax.random.key(seed), 12)
    first_guess = centred(arg_keys[0], (SAMPLES, WINDOW_DAYS, LON_CELLS, LAT_CELLS), 1.0, 6.0, ((1, 2), (2, 16)), jnp.float32)
    observed = centred(arg_keys[1], (SAMPLES, WINDOW_DAYS, LON_CELLS, LAT_CELLS), 1.0, 6.0, ((1, 2), (2, 16)), jnp.float32)
    obs_mask = set_ends((jax.random.randint(arg_keys[2], (SAMPLES, WINDOW_DAYS, LON_CELLS, LAT_CELLS), 0, 3) < 1).astype(jnp.int32), jax.random.fold_in(arg_keys[2], 1), 0, 1)
    land_mask = set_ends((jax.random.randint(arg_keys[3], (LON_CELLS, LAT_CELLS), 0, 5) < 4).astype(jnp.int32), jax.random.fold_in(arg_keys[3], 1), 0, 1)
    enc_weight = centred(arg_keys[4], (PRIOR_CH, 27), 27 ** -0.5, 1.25, (), jnp.float32)
    enc_bias = jnp.clip(jax.random.uniform(arg_keys[5], (PRIOR_CH,), jnp.float32, -0.5, 0.5), -0.5, 0.5)
    dec_weight = centred(arg_keys[6], (PRIOR_CH, 27), (27 * PRIOR_CH) ** -0.5, 0.21875, (), jnp.float32)
    dec_bias = jnp.clip(jax.random.uniform(arg_keys[7], (1,), jnp.float32, -1.0, 1.0), -1.0, 1.0)
    gate_weight = centred(arg_keys[8], (GATE_CH, 9 * (STATE_CH + 1)), (9 * (STATE_CH + 1)) ** -0.5, 0.25)
    gate_bias = jnp.clip(jax.random.uniform(arg_keys[9], (GATE_CH,), jnp.float32, -1.0, 1.0), -1.0, 1.0)
    out_weight = centred(arg_keys[10], (STATE_CH,), STATE_CH ** -0.5, 0.875, (), jnp.float32)
    return {"first_guess": first_guess, "observed": observed, "obs_mask": obs_mask, "land_mask": land_mask, "enc_weight": enc_weight, "enc_bias": enc_bias, "dec_weight": dec_weight, "dec_bias": dec_bias, "gate_weight": gate_weight, "gate_bias": gate_bias, "out_weight": out_weight}


exact_mode = lax.Precision.HIGHEST
tap_offsets = [(first, second, third) for first in range(3) for second in range(3) for third in range(3)]
plane_offsets = [(second, third) for second in range(3) for third in range(3)]


def pad_lat(grid_field):
    return jnp.pad(grid_field, [(0, 0)] * (grid_field.ndim - 1) + [(1, 1)])


def pad_cycle(grid_field):
    wrapped = jnp.concatenate([grid_field[..., -1:, :], grid_field, grid_field[..., :1, :]], axis=-2)
    return jnp.pad(wrapped, [(0, 0)] * (grid_field.ndim - 3) + [(1, 1), (0, 0), (0, 0)])


def lift_local(wide_field, span_day, span_lon, weight, flipped):
    lat_count = wide_field.shape[-1]
    padded = pad_lat(wide_field)
    pieces = []
    for first, second, third in tap_offsets:
        if flipped:
            first, second, third = 2 - first, 2 - second, 2 - third
        pieces.append(padded[first:first + span_day, second:second + span_lon, third:third + lat_count])
    columns = jnp.stack(pieces)
    return jnp.einsum("ck,ktlz->ctlz", weight, columns, precision=exact_mode)


def spread_local(channels, span_day, span_lon, weight, flipped):
    lat_count = channels.shape[-1]
    projected = jnp.einsum("ck,ctlz->ktlz", weight, pad_lat(channels), precision=exact_mode)
    accum = jnp.zeros((span_day, span_lon, lat_count), jnp.float32)
    for index, (first, second, third) in enumerate(tap_offsets):
        if flipped:
            first, second, third = 2 - first, 2 - second, 2 - third
        accum = accum + projected[index, first:first + span_day, second:second + span_lon, third:third + lat_count]
    return accum


def reference(first_guess, observed, obs_mask, land_mask, enc_weight, enc_bias, dec_weight, dec_bias, gate_weight, gate_bias, out_weight):
    sea_cells = land_mask.astype(jnp.float32)

    def solve_one(pieces):
        estimate, target, seen_raw = pieces
        seen_mask = seen_raw.astype(jnp.float32)
        day_count, lon_count, lat_count = estimate.shape
        state_hidden = jnp.zeros((STATE_CH,) + estimate.shape, jnp.float32)
        state_cell = jnp.zeros((STATE_CH,) + estimate.shape, jnp.float32)
        for iteration in range(SOLVER_ITERS):
            encoded = lift_local(pad_cycle(estimate), day_count, lon_count, enc_weight, False) + enc_bias[:, None, None, None]
            activated = jnp.maximum(encoded, 0.0)
            rebuilt = spread_local(pad_cycle(activated), day_count, lon_count, dec_weight, False) + dec_bias[0]
            misfit = sea_cells * (estimate - rebuilt)
            lifted = lift_local(pad_cycle(misfit), day_count, lon_count, dec_weight, True)
            back_hidden = jnp.where(encoded > 0, lifted, 0.0)
            back = spread_local(pad_cycle(back_hidden), day_count, lon_count, enc_weight, True)
            gradient = 2.0 * seen_mask * (estimate - target) + misfit - back
            stacked = jnp.concatenate([gradient[None], state_hidden], axis=0).astype(jnp.bfloat16)
            wrapped = jnp.concatenate([stacked[:, :, -1:], stacked, stacked[:, :, :1]], axis=2)
            padded = pad_lat(wrapped)
            in_count = stacked.shape[0]
            gate_sums = jnp.zeros((gate_weight.shape[0], day_count * lon_count * lat_count), jnp.float32)
            for index, (second, third) in enumerate(plane_offsets):
                piece = padded[:, :, second:second + lon_count, third:third + lat_count].reshape(in_count, -1)
                gate_sums = gate_sums + jnp.dot(gate_weight[:, index * in_count:(index + 1) * in_count], piece, preferred_element_type=jnp.float32)
            gate_sums = (gate_sums + gate_bias[:, None]).reshape((gate_weight.shape[0],) + estimate.shape)
            input_gate = jax.nn.sigmoid(gate_sums[:STATE_CH])
            forget_gate = jax.nn.sigmoid(gate_sums[STATE_CH:2 * STATE_CH])
            cell_input = jnp.tanh(gate_sums[2 * STATE_CH:3 * STATE_CH])
            output_gate = jax.nn.sigmoid(gate_sums[3 * STATE_CH:])
            state_cell = forget_gate * state_cell + input_gate * cell_input
            state_hidden = output_gate * jnp.tanh(state_cell)
            estimate = estimate - jnp.einsum("c,ctlz->tlz", out_weight, state_hidden, precision=exact_mode)
        return estimate

    return lax.map(solve_one, (first_guess, observed, obs_mask))
```

```python
import functools

import jax
import jax.numpy as jnp
from jax import lax
from jax.experimental import pallas as pl
from jax.experimental.pallas import tpu as pltpu
from jax.sharding import PartitionSpec as P

SOLVER_ITERS = 2
HALO_DAYS = 4
SLOT = 8
EDGE = 4
MESH = pl.DeviceIdType.MESH
F32, BF16 = jnp.float32, jnp.bfloat16


def up(n, m):
    return (n + m - 1) // m * m


def iota(shape, dim):
    return lax.broadcasted_iota(jnp.int32, shape, dim)


def halves(v):
    hi = v.astype(BF16)
    return hi, (v - hi.astype(F32)).astype(BF16)


def mm(a, b):
    return jnp.dot(a, b, preferred_element_type=F32)


def mm3(ahi, alo, bhi, blo):
    return mm(ahi, bhi) + mm(ahi, blo) + mm(alo, bhi)


def column(row):
    n = row.shape[1]
    eye = iota((n, n), 0) == iota((n, n), 1)
    return jnp.sum(jnp.where(eye, jnp.broadcast_to(row, (n, n)), 0.0), axis=1, keepdims=True)


def shifts(v):
    lanes = v.shape[-1]
    lane = iota(v.shape, v.ndim - 1)
    lower = jnp.where(lane == 0, 0.0, pltpu.roll(v, 1, v.ndim - 1))
    upper = jnp.where(lane == lanes - 1, 0.0, pltpu.roll(v, lanes - 1, v.ndim - 1))
    return lower, v, upper


def tap(a, b, c, flip):
    k = 9 * a + 3 * b + c
    return 26 - k if flip else k


def build_lift(w, hi_ref, lo_ref, outs, rows_in, day_rows, offset, flip, bias=None):
    ch = w.shape[0]
    width = hi_ref.shape[1]
    q = iota((ch, width), 1)
    row = jnp.full((ch, width), -1000, jnp.int32)
    taps = [jnp.zeros((ch, width), F32) for _ in range(3)]
    for a in range(3):
        for c in range(3):
            base = a * day_rows + c * rows_in
            inside = (q >= base) & (q < base + rows_in)
            row = jnp.where(inside, q - base, row)
            for b in range(3):
                k = tap(a, b, c, flip)
                taps[b] = jnp.where(inside, w[:, k : k + 1], taps[b])
    start = jnp.zeros((ch, width), F32)
    if bias is not None:
        start = jnp.where(q == 3 * rows_in, bias, start)
    for j in range(outs):
        acc = start
        for b in range(3):
            acc = jnp.where(row == j + offset + b, taps[b], acc)
        hi, lo = halves(acc)
        hi_ref[j * ch : (j + 1) * ch, :] = hi
        lo_ref[j * ch : (j + 1) * ch, :] = lo


def build_spread(w, hi_ref, lo_ref, rows_out, first, count, flip):
    ch = w.shape[0]
    width = count * ch
    eye = (iota((27, 27), 0) == iota((27, 27), 1)).astype(BF16)
    lane = iota((rows_out, width), 1)
    col = jnp.full((rows_out, width), first, jnp.int32)
    for i in range(1, count):
        col = col + (lane >= i * ch).astype(jnp.int32)
    where_b = col - iota((rows_out, width), 0) + 1
    for part, ref in zip(halves(w), (hi_ref, lo_ref)):
        tiled = jnp.concatenate([part.astype(F32)] * count, axis=0).astype(BF16)
        flat = lax.dot_general(eye, tiled, (((1,), (1,)), ((), ())), preferred_element_type=F32)
        for a in range(3):
            for c in range(3):
                acc = jnp.zeros((rows_out, width), F32)
                for b in range(3):
                    k = tap(a, b, c, flip)
                    acc = jnp.where(where_b == b, flat[k : k + 1, :], acc)
                at = (a * 3 + c) * rows_out
                ref[at : at + rows_out, :] = acc.astype(BF16)


def kernel(
    n_t, n_l, D, L, C, S,
    x_ref, y_ref, m_ref, land_ref, ew_ref, eb_ref, dw_ref, db_ref, gw_ref, gb_ref, ow_ref,
    out_ref,
    xr, yr, mr, lr, xs_hi, xs_lo, ms_hi, ms_lo, act, pb, qb, mis_ref, g3, h3, hs, hr, cell,
    te_hi, te_lo, td_hi, td_lo, se_hi, se_lo, sd_hi, sd_lo, gwt, wst, gst,
    send, recv,
):
    N = x_ref.shape[-1]
    R = L + 2 * SLOT
    E = L + 2 * EDGE
    B = E - 4
    KX = up(3 * R + 1, 16)
    KM = up(3 * E, 16)
    KG = up(3 * E + 3, 16)
    WX, WM, WG = te_hi.shape[1], td_hi.shape[1], gwt.shape[2]
    WS = wst.shape[1]
    total = n_t * D
    W = min(total, D + 2 * HALO_DAYS)
    HALF = D // 2
    t = lax.axis_index("tm")
    l = lax.axis_index("lon")
    right = lax.rem(l + 1, n_l)
    left = lax.rem(l + n_l - 1, n_l)

    def window(tt):
        return jnp.clip(tt * D - HALO_DAYS, 0, total - W)

    o = t * D - window(t)

    if n_t > 2:
        xr[...] = jnp.zeros_like(xr)

    barrier = pltpu.get_barrier_semaphore()
    moves = [(dt, dl) for dt in (0, -1, 1) for dl in (-1, 1, 0) if (dt, dl) != (0, 0)]

    def target(dt, dl):
        return (t + dt, {-1: left, 0: l, 1: right}[dl])

    def guarded(dt, fn):
        if dt == 0:
            fn()
        else:
            pl.when((t + dt >= 0) & (t + dt < n_t))(fn)

    for dt, dl in moves:
        def greet(dt=dt, dl=dl):
            pl.semaphore_signal(barrier, inc=1, device_id=target(dt, dl), device_id_type=MESH)
        guarded(dt, greet)
    around = 2 + 3 * ((t > 0).astype(jnp.int32) + (t < n_t - 1).astype(jnp.int32))
    pl.semaphore_wait(barrier, around)

    def src_lon(dl):
        return {-1: pl.ds(0, SLOT), 0: pl.ds(0, L), 1: pl.ds(L - SLOT, SLOT)}[dl]

    def dst_lon(dl):
        return {-1: pl.ds(SLOT + L, SLOT), 0: pl.ds(SLOT, L), 1: pl.ds(0, SLOT)}[dl]

    def x_copy(it, src, base_day, base_lon, dt, dl, index, sender):
        first = {-1: 0, 0: 0, 1: D - HALO_DAYS}[dt]
        days = D if dt == 0 else HALO_DAYS
        day = sender * D + first - window(sender + dt)
        lon = src_lon(dl)
        source = src.at[pl.ds(base_day + first, days), pl.ds(base_lon + lon.start, lon.size), :]
        return pltpu.make_async_remote_copy(
            src_ref=source,
            dst_ref=xr.at[it, pl.ds(day, days), dst_lon(dl), :],
            send_sem=send.at[index], recv_sem=recv.at[index],
            device_id=target(dt, dl), device_id_type=MESH,
        )

    def plain_copy(src, dst, dl, index):
        return pltpu.make_async_remote_copy(
            src_ref=src, dst_ref=dst, send_sem=send.at[index], recv_sem=recv.at[index],
            device_id=target(0, dl), device_id_type=MESH,
        )

    def x_start(it, src, base_day, base_lon, slot0):
        for i, (dt, dl) in enumerate(moves):
            def go(i=i, dt=dt, dl=dl):
                x_copy(it, src, base_day, base_lon, dt, dl, slot0 + i, t).start()
            guarded(dt, go)

    def x_wait(it, src, base_day, base_lon, slot0):
        for i, (dt, dl) in enumerate(moves):
            def got(i=i, dt=dt, dl=dl):
                x_copy(it, src, base_day, base_lon, dt, dl, slot0 + i, t - dt).wait_recv()
            def sent(i=i, dt=dt, dl=dl):
                x_copy(it, src, base_day, base_lon, dt, dl, slot0 + i, t).wait_send()
            guarded(-dt, got)
            guarded(dt, sent)

    x_start(0, x_ref, 0, 0, 0)
    others = []
    for i, dl in enumerate((-1, 1)):
        others.append(plain_copy(y_ref.at[:, src_lon(dl), :], yr.at[:, dst_lon(dl), :], dl, 8 + i))
        others.append(plain_copy(m_ref.at[:, src_lon(dl), :], mr.at[:, dst_lon(dl), :], dl, 10 + i))
        others.append(plain_copy(land_ref.at[src_lon(dl), :], lr.at[dst_lon(dl), :], dl, 12 + i))
    for copy in others:
        copy.start()

    own = pl.ds(SLOT, L)
    xr[0, pl.ds(o, D), own, :] = x_ref[...]
    yr[:, own, :] = y_ref[...]
    mr[:, own, :] = m_ref[...]
    lr[own, :] = land_ref[...]
    for ref in (ms_hi, ms_lo, pb, qb, g3):
        ref[...] = jnp.zeros_like(ref)
    for ref in (xs_hi, xs_lo):
        ref[0 : KX, :] = jnp.zeros((KX, N), BF16)
        ref[(W + 1) * KX :, :] = jnp.zeros((ref.shape[0] - (W + 1) * KX, N), BF16)
    tail = (iota((KX - 3 * R, N), 0) == 0).astype(F32)
    xs_hi[0 : KX, :] = jnp.concatenate([jnp.zeros((3 * R, N), F32), tail], axis=0).astype(BF16)
    h3[D * (L + 2) * 3 * S :, :] = jnp.zeros((h3.shape[0] - D * (L + 2) * 3 * S, N), BF16)
    for d in range(D):
        at = (d * (L + 2) + L + 1) * 3 * S
        h3[at : at + 3 * S, :] = jnp.zeros((3 * S, N), BF16)

    ew, dw = ew_ref[...], dw_ref[...]
    build_lift(ew, te_hi, te_lo, E, R, KX, SLOT - EDGE - 1, False, column(eb_ref[...]))
    build_spread(dw, sd_hi, sd_lo, E, 0, E, False)
    build_lift(dw, td_hi, td_lo, B, E, KM, 1, True)
    build_spread(ew, se_hi, se_lo, E, 2, B, True)

    wide = gw_ref[...].astype(F32)
    gate_rows = iota((4 * S, 1), 0)
    scale = jnp.where((gate_rows >= 2 * S) & (gate_rows < 3 * S), 1.0, 0.5)
    wide = wide * scale
    gbias = column(gb_ref[...]) * scale
    b_hi, b_rest = gbias.astype(BF16), None
    b_rest = gbias - b_hi.astype(F32)
    b_mid = b_rest.astype(BF16).astype(F32)
    b_low = b_rest - b_mid
    ins = S + 1
    q = iota((4 * S, WG), 1)
    start = jnp.where(q == 3 * E, b_hi.astype(F32), 0.0)
    start = jnp.where(q == 3 * E + 1, b_mid, start)
    start = jnp.where(q == 3 * E + 2, b_low, start)
    row = jnp.full((4 * S, WG), -1000, jnp.int32)
    taps = [jnp.zeros((4 * S, WG), F32) for _ in range(3)]
    for c in range(3):
        inside = (q >= c * E) & (q < (c + 1) * E)
        row = jnp.where(inside, q - c * E, row)
        for b in range(3):
            k = (3 * b + c) * ins
            taps[b] = jnp.where(inside, wide[:, k : k + 1], taps[b])
    for j in range(L):
        acc = start
        for b in range(3):
            acc = jnp.where(row == j + EDGE - 1 + b, taps[b], acc)
        gwt[j] = acc.astype(BF16)

    oweight = jnp.broadcast_to(column(ow_ref[...]), (S, 2 * N))
    dbias = db_ref[0]

    def finish(parts):
        lower, mid, upper = parts
        lane = iota(lower.shape, 1)
        return (
            jnp.where(lane == 0, 0.0, pltpu.roll(lower, 1, 1))
            + mid
            + jnp.where(lane == N - 1, 0.0, pltpu.roll(upper, N - 1, 1))
        )

    def gather_taps(ref, d):
        parts = []
        for c in range(3):
            parts.append(
                ref[d, c * E : (c + 1) * E, :]
                + ref[d + 1, (3 + c) * E : (4 + c) * E, :]
                + ref[d + 2, (6 + c) * E : (7 + c) * E, :]
            )
        return finish(parts)

    def pair(ref, d, rows, width):
        return jnp.concatenate(
            [ref[pl.ds(pl.multiple_of((d + i) * rows, 16), width), :] for i in range(2)], axis=1
        )

    def span(radius):
        n = min(W, D + 2 * radius)
        return jnp.clip(o - radius, 0, W - n), n

    edge_rows = pl.ds(SLOT - EDGE, E)

    def gradient(it):
        def stage_x(d, carry):
            f = xr[it, d]
            low, mid, high = shifts(f)
            v = jnp.concatenate([low, mid, high, tail], axis=0)
            hi, lo = halves(v)
            at = pl.ds(pl.multiple_of((d + 1) * KX, 16), KX)
            xs_hi[at, :] = hi
            xs_lo[at, :] = lo
            return carry

        lax.fori_loop(0, W, stage_x, 0)

        s3, n3 = span(3)

        def encode(p, carry):
            d = s3 + 2 * p
            enc = mm3(te_hi[...], te_lo[...], pair(xs_hi, d, KX, WX), pair(xs_lo, d, KX, WX))
            hi, lo = halves(jnp.maximum(enc, 0.0))
            out = mm3(sd_hi[...], sd_lo[...], hi, lo)
            for i in range(2):
                act[d + i] = hi[2 * C : (2 + B) * C, i * N : (i + 1) * N]
                pb[d + i + 1] = out[:, i * N : (i + 1) * N]
            return carry

        lax.fori_loop(0, n3 // 2, encode, 0)

        s2, n2 = span(2)
        sea = lr[edge_rows, :].astype(F32)

        def misfit(i, carry):
            d = s2 + i
            rebuilt = gather_taps(pb, d) + dbias
            mis = sea * (xr[it, d, edge_rows, :] - rebuilt)
            mis_ref[d] = mis
            parts = list(shifts(mis))
            if KM > 3 * E:
                parts.append(jnp.zeros((KM - 3 * E, N), F32))
            hi, lo = halves(jnp.concatenate(parts, axis=0))
            at = pl.ds(pl.multiple_of((d + 1) * KM, 16), KM)
            ms_hi[at, :] = hi
            ms_lo[at, :] = lo
            return carry

        lax.fori_loop(0, n2, misfit, 0)

        s1, n1 = span(1)

        def backward(p, carry):
            d = s1 + 2 * p
            lifted = mm3(td_hi[...], td_lo[...], pair(ms_hi, d, KM, WM), pair(ms_lo, d, KM, WM))
            on = jnp.concatenate([act[d], act[d + 1]], axis=1).astype(F32)
            hi, lo = halves(jnp.where(on > 0.0, lifted, 0.0))
            out = mm3(se_hi[...], se_lo[...], hi, lo)
            for i in range(2):
                qb[d + i + 1] = out[:, i * N : (i + 1) * N]
            return carry

        lax.fori_loop(0, n1 // 2, backward, 0)

        ones = (iota((KG - 3 * E, N), 0) < 3).astype(F32)

        def collect(i, carry):
            d = o + i
            back = gather_taps(qb, d)
            seen = mr[i, edge_rows, :].astype(F32)
            grad = (
                2.0 * seen * (xr[it, d, edge_rows, :] - yr[i, edge_rows, :]) + mis_ref[d] - back
            )
            v = jnp.concatenate(list(shifts(grad)) + [ones], axis=0)
            g3[pl.ds(pl.multiple_of(i * KG, 16), KG), :] = v.astype(BF16)
            return carry

        lax.fori_loop(0, D, collect, 0)

    def sig(v):
        return 0.5 * jnp.tanh(v) + 0.5

    def h_copies():
        return [
            plain_copy(hs.at[0], hr.at[1], -1, 22),
            plain_copy(hs.at[1], hr.at[0], 1, 23),
        ]

    def put_h3(d, lon, h):
        v = jnp.concatenate(list(shifts(h)), axis=0).astype(BF16)
        h3[pl.ds(pl.multiple_of((d * (L + 2) + lon) * 3 * S, 16), 3 * S), :] = v

    for copy in others:
        copy.wait()
    x_wait(0, x_ref, 0, 0, 0)
    gradient(0)

    def first_gates(j, carry):
        for p in range(HALF):
            rhs = pair(g3, 2 * p, KG, WG)
            up_ = mm(gwt[j, 0:S, :], rhs)
            rest = mm(gwt[j, 2 * S : 4 * S, :], rhs)
            state = sig(up_) * jnp.tanh(rest[0:S])
            hidden = sig(rest[S : 2 * S]) * jnp.tanh(state)
            cell[j, p] = state
            step = jnp.sum(oweight * hidden, axis=0, keepdims=True)
            for i in range(2):
                d = 2 * p + i
                h = hidden[:, i * N : (i + 1) * N]
                put_h3(d, j + 1, h)
                at = pl.ds(SLOT + j, 1)
                xr[1, o + d, at, :] = xr[0, o + d, at, :] - step[:, i * N : (i + 1) * N]
                for side, lon in ((0, 0), (1, L - 1)):
                    @pl.when(j == lon)
                    def _(side=side, d=d, h=h):
                        hs[side, d] = h.astype(BF16)
        return carry

    lax.fori_loop(0, L, first_gates, 0)
    x_start(1, xr.at[1], o, SLOT, 14)
    for copy in h_copies():
        copy.start()

    for base in range(0, WS, 128):
        src = iota((9 * ins, 128), 0)
        lane = iota((9 * ins, 128), 1) + base
        want = lane + 1
        for i in range(1, 9):
            want = want + (lane >= i * S).astype(jnp.int32)
        pick = ((src == want) & (lane < 9 * S)).astype(F32).astype(BF16)
        wst[:, base : base + 128] = mm(wide.astype(BF16), pick).astype(BF16)

    def state_part(j):
        for p in range(HALF):
            rhs = jnp.concatenate(
                [
                    h3[pl.ds(pl.multiple_of(((2 * p + i) * (L + 2) + j) * 3 * S, 16), WS), :]
                    for i in range(2)
                ],
                axis=1,
            )
            gst[j, p] = mm(wst[...], rhs)

    def inner(j, carry):
        state_part(j)
        return carry

    lax.fori_loop(1, L - 1, inner, 0)
    for copy in h_copies():
        copy.wait()
    for d in range(D):
        put_h3(d, 0, hr[0, d].astype(F32))
        put_h3(d, L + 1, hr[1, d].astype(F32))
    state_part(0)
    state_part(L - 1)
    x_wait(1, xr.at[1], o, SLOT, 14)
    gradient(1)

    def last_gates(j, carry):
        for p in range(HALF):
            rhs = pair(g3, 2 * p, KG, WG)
            sums = gst[j, p] + mm(gwt[j], rhs)
            state = sig(sums[S : 2 * S]) * cell[j, p] + sig(sums[0:S]) * jnp.tanh(
                sums[2 * S : 3 * S]
            )
            hidden = sig(sums[3 * S :]) * jnp.tanh(state)
            step = jnp.sum(oweight * hidden, axis=0, keepdims=True)
            for i in range(2):
                d = 2 * p + i
                out_ref[d, pl.ds(j, 1), :] = (
                    xr[1, o + d, pl.ds(SLOT + j, 1), :] - step[:, i * N : (i + 1) * N]
                )
        return carry

    lax.fori_loop(0, L, last_gates, 0)


def body(n_t, n_l, x, y, m, land, ew, eb, dw, db, gw, gb, ow):
    D, L, N = x.shape[1:]
    C = eb.shape[0]
    S = ow.shape[0]
    R, E = L + 2 * SLOT, L + 2 * EDGE
    B = E - 4
    W = min(n_t * D, D + 2 * HALO_DAYS)
    KX, KM, KG = up(3 * R + 1, 16), up(3 * E, 16), up(3 * E + 3, 16)
    WX, WM, WG, WS = up(3 * KX, 128), up(3 * KM, 128), up(KG, 128), up(9 * S, 128)
    G = 4 * S
    vm = pltpu.VMEM
    scratch = [
        vm((2, W, R, N), F32), vm((D, R, N), F32), vm((D, R, N), jnp.int32), vm((R, N), jnp.int32),
        vm(((W + 2) * KX + WX - 3 * KX, N), BF16), vm(((W + 2) * KX + WX - 3 * KX, N), BF16),
        vm(((W + 2) * KM + WM - 3 * KM, N), BF16), vm(((W + 2) * KM + WM - 3 * KM, N), BF16),
        vm((W, B * C, N), BF16), vm((W + 2, 9 * E, N), F32), vm((W + 2, 9 * E, N), F32),
        vm((W, E, N), F32), vm((D * KG + WG - KG, N), BF16),
        vm((D * (L + 2) * 3 * S + WS - 9 * S, N), BF16),
        vm((2, D, S, N), BF16), vm((2, D, S, N), BF16), vm((L, D // 2, S, 2 * N), F32),
        vm((E * C, WX), BF16), vm((E * C, WX), BF16), vm((B * C, WM), BF16), vm((B * C, WM), BF16),
        vm((9 * E, B * C), BF16), vm((9 * E, B * C), BF16),
        vm((9 * E, E * C), BF16), vm((9 * E, E * C), BF16),
        vm((L, G, WG), BF16), vm((G, WS), BF16), vm((L, D // 2, G, 2 * N), F32),
        pltpu.SemaphoreType.DMA((24,)), pltpu.SemaphoreType.DMA((24,)),
    ]
    v = pl.BlockSpec(memory_space=pltpu.VMEM)
    specs = [v] * 7 + [pl.BlockSpec(memory_space=pltpu.SMEM)] + [v] * 3
    out = pl.pallas_call(
        functools.partial(kernel, n_t, n_l, D, L, C, S),
        out_shape=jax.ShapeDtypeStruct((D, L, N), F32),
        in_specs=specs,
        out_specs=v,
        scratch_shapes=scratch,
        compiler_params=pltpu.CompilerParams(
            collective_id=0, has_side_effects=True, vmem_limit_bytes=48 << 20
        ),
        name="solver",
    )(x[0], y[0], m[0], land, ew, eb[None], dw, db, gw, gb[None], ow[None])
    return out[None]


def solution(mesh):
    tile = P(None, "tm", "lon", None)
    run = functools.partial(body, mesh.shape["tm"], mesh.shape["lon"])
    return jax.shard_map(
        run, mesh=mesh, in_specs=(tile, tile, tile, P("lon", None)) + (P(),) * 7,
        out_specs=tile, check_vma=False,
    )
```

```python
import functools

import jax
import jax.numpy as jnp
from jax import lax
from jax.experimental import pallas as pl
from jax.experimental.pallas import tpu as pltpu
from jax.sharding import PartitionSpec as P

SOLVER_ITERS = 2
HALO_DAYS = 4
SLOT = 8
EDGE = 4
MESH = pl.DeviceIdType.MESH
F32, BF16 = jnp.float32, jnp.bfloat16


def up(n, m):
    return (n + m - 1) // m * m


def iota(shape, dim):
    return lax.broadcasted_iota(jnp.int32, shape, dim)


def halves(v):
    hi = v.astype(BF16)
    return hi, (v - hi.astype(F32)).astype(BF16)


def mm(a, b):
    return jnp.dot(a, b, preferred_element_type=F32)


def mm3(ahi, alo, bhi, blo):
    return mm(ahi, bhi) + mm(ahi, blo) + mm(alo, bhi)


def column(row):
    n = row.shape[1]
    eye = iota((n, n), 0) == iota((n, n), 1)
    return jnp.sum(jnp.where(eye, jnp.broadcast_to(row, (n, n)), 0.0), axis=1, keepdims=True)


def shifts(v):
    lanes = v.shape[-1]
    lane = iota(v.shape, v.ndim - 1)
    lower = jnp.where(lane == 0, 0.0, pltpu.roll(v, 1, v.ndim - 1))
    upper = jnp.where(lane == lanes - 1, 0.0, pltpu.roll(v, lanes - 1, v.ndim - 1))
    return lower, v, upper


def tap(a, b, c, flip):
    k = 9 * a + 3 * b + c
    return 26 - k if flip else k


def build_lift(w, hi_ref, lo_ref, outs, rows_in, day_rows, offset, flip, bias=None):
    ch = w.shape[0]
    width = hi_ref.shape[1]
    q = iota((ch, width), 1)
    row = jnp.full((ch, width), -1000, jnp.int32)
    taps = [jnp.zeros((ch, width), F32) for _ in range(3)]
    for a in range(3):
        for c in range(3):
            base = a * day_rows + c * rows_in
            inside = (q >= base) & (q < base + rows_in)
            row = jnp.where(inside, q - base, row)
            for b in range(3):
                k = tap(a, b, c, flip)
                taps[b] = jnp.where(inside, w[:, k : k + 1], taps[b])
    start = jnp.zeros((ch, width), F32)
    if bias is not None:
        start = jnp.where(q == 3 * rows_in, bias, start)
    for j in range(outs):
        acc = start
        for b in range(3):
            acc = jnp.where(row == j + offset + b, taps[b], acc)
        hi, lo = halves(acc)
        hi_ref[j * ch : (j + 1) * ch, :] = hi
        if lo_ref is not None:
            lo_ref[j * ch : (j + 1) * ch, :] = lo


def build_spread(w, out_ref, rows_out, first, count, flip):
    ch = w.shape[0]
    width = count * ch
    eye = (iota((27, 27), 0) == iota((27, 27), 1)).astype(BF16)
    lane = iota((rows_out, width), 1)
    col = jnp.full((rows_out, width), first, jnp.int32)
    for i in range(1, count):
        col = col + (lane >= i * ch).astype(jnp.int32)
    where_b = col - iota((rows_out, width), 0) + 1
    tiled = jnp.concatenate([w] * count, axis=0).astype(BF16)
    flat = lax.dot_general(eye, tiled, (((1,), (1,)), ((), ())), preferred_element_type=F32)
    for a in range(3):
        for c in range(3):
            acc = jnp.zeros((rows_out, width), F32)
            for b in range(3):
                k = tap(a, b, c, flip)
                acc = jnp.where(where_b == b, flat[k : k + 1, :], acc)
            at = (a * 3 + c) * rows_out
            out_ref[at : at + rows_out, :] = acc.astype(BF16)


def kernel(
    n_t, n_l, D, L, C, S,
    x_ref, y_ref, m_ref, land_ref, *rest,
):
    weights, out_ref, filled = rest[:7], rest[7], rest[8:15]
    kernel_body(
        n_t, n_l, D, L, C, S, x_ref, y_ref, m_ref, land_ref, weights, filled, out_ref, *rest[15:]
    )


def kernel_body(
    n_t, n_l, D, L, C, S,
    x_ref, y_ref, m_ref, land_ref, weights, filled, out_ref,
    xr, yr, mr, lr, xs_hi, xs_lo, ms, act, pb, qb, mis_ref, g3, h3, hs, hr, cell,
    te_hi, te_lo, td, se, sd, gwt, wst, gst,
    send, recv, local,
):
    N = x_ref.shape[-1]
    R = L + 2 * SLOT
    E = L + 2 * EDGE
    B = E - 4
    KX = up(3 * R + 1, 16)
    KM = up(3 * E, 16)
    KG = up(3 * E + 3, 16)
    WX, WM, WG = te_hi.shape[1], td.shape[1], gwt.shape[2]
    WS = wst.shape[1]
    total = n_t * D
    W = min(total, D + 2 * HALO_DAYS)
    HALF = D // 2
    t = lax.axis_index("tm")
    l = lax.axis_index("lon")
    right = lax.rem(l + 1, n_l)
    left = lax.rem(l + n_l - 1, n_l)

    def window(tt):
        return jnp.clip(tt * D - HALO_DAYS, 0, total - W)

    o = t * D - window(t)

    own = pl.ds(SLOT, L)
    ew_ref, eb_ref, dw_ref, db_ref, gw_ref, gb_ref, ow_ref = filled
    fetches = [
        pltpu.make_async_copy(a, b, local.at[i]) for i, (a, b) in enumerate(zip(weights, filled))
    ]
    for copy in fetches:
        copy.start()

    if n_t > 2:
        xr[...] = jnp.zeros_like(xr)

    barrier = pltpu.get_barrier_semaphore()
    moves = [(dt, dl) for dt in (0, -1, 1) for dl in (-1, 1, 0) if (dt, dl) != (0, 0)]

    def target(dt, dl):
        return (t + dt, {-1: left, 0: l, 1: right}[dl])

    def guarded(dt, fn):
        if dt == 0:
            fn()
        else:
            pl.when((t + dt >= 0) & (t + dt < n_t))(fn)

    for dt, dl in moves:
        def greet(dt=dt, dl=dl):
            pl.semaphore_signal(barrier, inc=1, device_id=target(dt, dl), device_id_type=MESH)
        guarded(dt, greet)
    around = 2 + 3 * ((t > 0).astype(jnp.int32) + (t < n_t - 1).astype(jnp.int32))
    pl.semaphore_wait(barrier, around)

    def src_lon(dl):
        return {-1: pl.ds(0, SLOT), 0: pl.ds(0, L), 1: pl.ds(L - SLOT, SLOT)}[dl]

    def dst_lon(dl):
        return {-1: pl.ds(SLOT + L, SLOT), 0: pl.ds(SLOT, L), 1: pl.ds(0, SLOT)}[dl]

    def x_copy(it, src, base_day, base_lon, dt, dl, index, sender):
        first = {-1: 0, 0: 0, 1: D - HALO_DAYS}[dt]
        days = D if dt == 0 else HALO_DAYS
        day = sender * D + first - window(sender + dt)
        lon = src_lon(dl)
        source = src.at[pl.ds(base_day + first, days), pl.ds(base_lon + lon.start, lon.size), :]
        return pltpu.make_async_remote_copy(
            src_ref=source,
            dst_ref=xr.at[it, pl.ds(day, days), dst_lon(dl), :],
            send_sem=send.at[index], recv_sem=recv.at[index],
            device_id=target(dt, dl), device_id_type=MESH,
        )

    def plain_copy(src, dst, dl, index):
        return pltpu.make_async_remote_copy(
            src_ref=src, dst_ref=dst, send_sem=send.at[index], recv_sem=recv.at[index],
            device_id=target(0, dl), device_id_type=MESH,
        )

    def x_start(it, src, base_day, base_lon, slot0):
        for i, (dt, dl) in enumerate(moves):
            def go(i=i, dt=dt, dl=dl):
                x_copy(it, src, base_day, base_lon, dt, dl, slot0 + i, t).start()
            guarded(dt, go)

    def x_wait(it, src, base_day, base_lon, slot0):
        for i, (dt, dl) in enumerate(moves):
            def got(i=i, dt=dt, dl=dl):
                x_copy(it, src, base_day, base_lon, dt, dl, slot0 + i, t - dt).wait_recv()
            def sent(i=i, dt=dt, dl=dl):
                x_copy(it, src, base_day, base_lon, dt, dl, slot0 + i, t).wait_send()
            guarded(-dt, got)
            guarded(dt, sent)

    x_start(0, x_ref, 0, 0, 0)
    others = []
    for i, dl in enumerate((-1, 1)):
        others.append(plain_copy(y_ref.at[:, src_lon(dl), :], yr.at[:, dst_lon(dl), :], dl, 8 + i))
        others.append(plain_copy(m_ref.at[:, src_lon(dl), :], mr.at[:, dst_lon(dl), :], dl, 10 + i))
        others.append(plain_copy(land_ref.at[src_lon(dl), :], lr.at[dst_lon(dl), :], dl, 12 + i))
    for copy in others:
        copy.start()

    tiles = [
        pltpu.make_async_copy(x_ref, xr.at[0, pl.ds(o, D), own, :], local.at[7]),
        pltpu.make_async_copy(y_ref, yr.at[:, own, :], local.at[8]),
        pltpu.make_async_copy(m_ref, mr.at[:, own, :], local.at[9]),
        pltpu.make_async_copy(land_ref, lr.at[own, :], local.at[10]),
    ]
    for copy in tiles:
        copy.start()
    for ref in (ms, pb, qb, g3):
        ref[...] = jnp.zeros_like(ref)
    for ref in (xs_hi, xs_lo):
        ref[0 : KX, :] = jnp.zeros((KX, N), BF16)
        ref[(W + 1) * KX :, :] = jnp.zeros((ref.shape[0] - (W + 1) * KX, N), BF16)
    tail = (iota((KX - 3 * R, N), 0) == 0).astype(F32)
    xs_hi[0 : KX, :] = jnp.concatenate([jnp.zeros((3 * R, N), F32), tail], axis=0).astype(BF16)
    h3[D * (L + 2) * 3 * S :, :] = jnp.zeros((h3.shape[0] - D * (L + 2) * 3 * S, N), BF16)
    for d in range(D):
        at = (d * (L + 2) + L + 1) * 3 * S
        h3[at : at + 3 * S, :] = jnp.zeros((3 * S, N), BF16)

    for copy in fetches:
        copy.wait()
    ew, dw = ew_ref[...], dw_ref[...]
    build_lift(ew, te_hi, te_lo, E, R, KX, SLOT - EDGE - 1, False, column(eb_ref[...]))
    build_spread(dw, sd, E, 0, E, False)
    build_lift(dw, td, None, B, E, KM, 1, True)
    build_spread(ew, se, E, 2, B, True)

    wide = gw_ref[...].astype(F32)
    gate_rows = iota((4 * S, 1), 0)
    scale = jnp.where((gate_rows >= 2 * S) & (gate_rows < 3 * S), 1.0, 0.5)
    wide = wide * scale
    gbias = column(gb_ref[...]) * scale
    b_hi, b_rest = gbias.astype(BF16), None
    b_rest = gbias - b_hi.astype(F32)
    b_mid = b_rest.astype(BF16).astype(F32)
    b_low = b_rest - b_mid
    ins = S + 1
    q = iota((4 * S, WG), 1)
    start = jnp.where(q == 3 * E, b_hi.astype(F32), 0.0)
    start = jnp.where(q == 3 * E + 1, b_mid, start)
    start = jnp.where(q == 3 * E + 2, b_low, start)
    row = jnp.full((4 * S, WG), -1000, jnp.int32)
    taps = [jnp.zeros((4 * S, WG), F32) for _ in range(3)]
    for c in range(3):
        inside = (q >= c * E) & (q < (c + 1) * E)
        row = jnp.where(inside, q - c * E, row)
        for b in range(3):
            k = (3 * b + c) * ins
            taps[b] = jnp.where(inside, wide[:, k : k + 1], taps[b])
    for j in range(L):
        acc = start
        for b in range(3):
            acc = jnp.where(row == j + EDGE - 1 + b, taps[b], acc)
        gwt[j] = acc.astype(BF16)

    for base in range(0, WS, 128):
        src = iota((9 * ins, 128), 0)
        lane = iota((9 * ins, 128), 1) + base
        want = lane + 1
        for i in range(1, 9):
            want = want + (lane >= i * S).astype(jnp.int32)
        pick = ((src == want) & (lane < 9 * S)).astype(F32).astype(BF16)
        wst[:, base : base + 128] = mm(wide.astype(BF16), pick).astype(BF16)

    oweight = jnp.broadcast_to(column(ow_ref[...]), (S, 2 * N))
    dbias = db_ref[0]

    def finish(parts):
        lower, mid, upper = parts
        lane = iota(lower.shape, 1)
        return (
            jnp.where(lane == 0, 0.0, pltpu.roll(lower, 1, 1))
            + mid
            + jnp.where(lane == N - 1, 0.0, pltpu.roll(upper, N - 1, 1))
        )

    def gather_taps(ref, d):
        parts = []
        for c in range(3):
            parts.append(
                ref[d, c * E : (c + 1) * E, :]
                + ref[d + 1, (3 + c) * E : (4 + c) * E, :]
                + ref[d + 2, (6 + c) * E : (7 + c) * E, :]
            )
        return finish(parts)

    def pair(ref, d, rows, width):
        return jnp.concatenate(
            [ref[pl.ds(pl.multiple_of((d + i) * rows, 16), width), :] for i in range(2)], axis=1
        )

    def span(radius):
        n = min(W, D + 2 * radius)
        return jnp.clip(o - radius, 0, W - n), n

    edge_rows = pl.ds(SLOT - EDGE, E)

    def gradient(it):
        def stage_x(d, carry):
            f = xr[it, d]
            low, mid, high = shifts(f)
            v = jnp.concatenate([low, mid, high, tail], axis=0)
            hi, lo = halves(v)
            at = pl.ds(pl.multiple_of((d + 1) * KX, 16), KX)
            xs_hi[at, :] = hi
            xs_lo[at, :] = lo
            return carry

        for i in range(W):
            stage_x(i, 0)

        s3, n3 = span(3)

        def encode(p, carry):
            d = s3 + 2 * p
            enc = mm3(te_hi[...], te_lo[...], pair(xs_hi, d, KX, WX), pair(xs_lo, d, KX, WX))
            hi = jnp.maximum(enc.astype(BF16), jnp.zeros((), BF16))
            out = mm(sd[...], hi)
            for i in range(2):
                act[d + i] = hi[2 * C : (2 + B) * C, i * N : (i + 1) * N]
                pb[d + i + 1] = out[:, i * N : (i + 1) * N]
            return carry

        for i in range(n3 // 2):
            encode(i, 0)

        s2, n2 = span(2)
        sea = lr[edge_rows, :].astype(F32)

        def misfit(i, carry):
            d = s2 + i
            rebuilt = gather_taps(pb, d) + dbias
            mis = sea * (xr[it, d, edge_rows, :] - rebuilt)
            mis_ref[d] = mis
            parts = list(shifts(mis))
            if KM > 3 * E:
                parts.append(jnp.zeros((KM - 3 * E, N), F32))
            at = pl.ds(pl.multiple_of((d + 1) * KM, 16), KM)
            ms[at, :] = jnp.concatenate(parts, axis=0).astype(BF16)
            return carry

        for i in range(n2):
            misfit(i, 0)

        s1, n1 = span(1)

        def backward(p, carry):
            d = s1 + 2 * p
            lifted = mm(td[...], pair(ms, d, KM, WM)).astype(BF16)
            on = jnp.concatenate([act[d], act[d + 1]], axis=1)
            zero = jnp.zeros((), BF16)
            out = mm(se[...], jnp.where(on > zero, lifted, zero))
            for i in range(2):
                qb[d + i + 1] = out[:, i * N : (i + 1) * N]
            return carry

        for i in range(n1 // 2):
            backward(i, 0)

        ones = (iota((KG - 3 * E, N), 0) < 3).astype(F32)

        def collect(i, carry):
            d = o + i
            back = gather_taps(qb, d)
            seen = mr[i, edge_rows, :].astype(F32)
            grad = (
                2.0 * seen * (xr[it, d, edge_rows, :] - yr[i, edge_rows, :]) + mis_ref[d] - back
            )
            v = jnp.concatenate(list(shifts(grad)) + [ones], axis=0)
            g3[pl.ds(pl.multiple_of(i * KG, 16), KG), :] = v.astype(BF16)
            return carry

        for i in range(D):
            collect(i, 0)

    def sig(v):
        return 0.5 * jnp.tanh(v) + 0.5

    def h_copies():
        return [
            plain_copy(hs.at[0], hr.at[1], -1, 22),
            plain_copy(hs.at[1], hr.at[0], 1, 23),
        ]

    def put_h3(d, lon, h):
        v = jnp.concatenate(list(shifts(h)), axis=0).astype(BF16)
        h3[pl.ds(pl.multiple_of((d * (L + 2) + lon) * 3 * S, 16), 3 * S), :] = v

    for copy in tiles + others:
        copy.wait()
    x_wait(0, x_ref, 0, 0, 0)
    gradient(0)

    def first_gates(j, carry):
        for p in range(HALF):
            rhs = pair(g3, 2 * p, KG, WG)
            up_ = mm(gwt[j, 0:S, :], rhs)
            rest = mm(gwt[j, 2 * S : 4 * S, :], rhs)
            state = sig(up_) * jnp.tanh(rest[0:S])
            hidden = sig(rest[S : 2 * S]) * jnp.tanh(state)
            cell[j, p] = state
            step = jnp.sum(oweight * hidden, axis=0, keepdims=True)
            for i in range(2):
                d = 2 * p + i
                h = hidden[:, i * N : (i + 1) * N]
                put_h3(d, j + 1, h)
                at = pl.ds(SLOT + j, 1)
                xr[1, o + d, at, :] = xr[0, o + d, at, :] - step[:, i * N : (i + 1) * N]
                for side, lon in ((0, 0), (1, L - 1)):
                    @pl.when(j == lon)
                    def _(side=side, d=d, h=h):
                        hs[side, d] = h.astype(BF16)
        return carry

    lax.fori_loop(0, L, first_gates, 0, unroll=4)
    x_start(1, xr.at[1], o, SLOT, 14)
    for copy in h_copies():
        copy.start()

    def state_part(j):
        for p in range(HALF):
            rhs = jnp.concatenate(
                [
                    h3[pl.ds(pl.multiple_of(((2 * p + i) * (L + 2) + j) * 3 * S, 16), WS), :]
                    for i in range(2)
                ],
                axis=1,
            )
            gst[j, p] = mm(wst[...], rhs)

    def inner(j, carry):
        state_part(j)
        return carry

    lax.fori_loop(1, L - 1, inner, 0, unroll=2)
    for copy in h_copies():
        copy.wait()
    for d in range(D):
        put_h3(d, 0, hr[0, d].astype(F32))
        put_h3(d, L + 1, hr[1, d].astype(F32))
    state_part(0)
    state_part(L - 1)
    x_wait(1, xr.at[1], o, SLOT, 14)
    gradient(1)

    def last_gates(j, carry):
        for p in range(HALF):
            rhs = pair(g3, 2 * p, KG, WG)
            sums = gst[j, p] + mm(gwt[j], rhs)
            state = sig(sums[S : 2 * S]) * cell[j, p] + sig(sums[0:S]) * jnp.tanh(
                sums[2 * S : 3 * S]
            )
            hidden = sig(sums[3 * S :]) * jnp.tanh(state)
            step = jnp.sum(oweight * hidden, axis=0, keepdims=True)
            for i in range(2):
                d = 2 * p + i
                out_ref[d, pl.ds(j, 1), :] = (
                    xr[1, o + d, pl.ds(SLOT + j, 1), :] - step[:, i * N : (i + 1) * N]
                )
        return carry

    lax.fori_loop(0, L, last_gates, 0, unroll=4)


def body(n_t, n_l, x, y, m, land, ew, eb, dw, db, gw, gb, ow):
    D, L, N = x.shape[1:]
    C = eb.shape[0]
    S = ow.shape[0]
    R, E = L + 2 * SLOT, L + 2 * EDGE
    B = E - 4
    W = min(n_t * D, D + 2 * HALO_DAYS)
    KX, KM, KG = up(3 * R + 1, 16), up(3 * E, 16), up(3 * E + 3, 16)
    WX, WM, WG, WS = up(3 * KX, 128), up(3 * KM, 128), up(KG, 128), up(9 * S, 128)
    G = 4 * S
    vm = pltpu.VMEM
    scratch = [
        vm((2, W, R, N), F32), vm((D, R, N), F32), vm((D, R, N), jnp.int32), vm((R, N), jnp.int32),
        vm(((W + 2) * KX + WX - 3 * KX, N), BF16), vm(((W + 2) * KX + WX - 3 * KX, N), BF16),
        vm(((W + 2) * KM + WM - 3 * KM, N), BF16),
        vm((W, B * C, N), BF16), vm((W + 2, 9 * E, N), F32), vm((W + 2, 9 * E, N), F32),
        vm((W, E, N), F32), vm((D * KG + WG - KG, N), BF16),
        vm((D * (L + 2) * 3 * S + WS - 9 * S, N), BF16),
        vm((2, D, S, N), BF16), vm((2, D, S, N), BF16), vm((L, D // 2, S, 2 * N), F32),
        vm((E * C, WX), BF16), vm((E * C, WX), BF16), vm((B * C, WM), BF16),
        vm((9 * E, B * C), BF16), vm((9 * E, E * C), BF16),
        vm((L, G, WG), BF16), vm((G, WS), BF16), vm((L, D // 2, G, 2 * N), F32),
        pltpu.SemaphoreType.DMA((24,)), pltpu.SemaphoreType.DMA((24,)), pltpu.SemaphoreType.DMA((11,)),
    ]
    v = pl.BlockSpec(memory_space=pltpu.VMEM)
    whole = pl.BlockSpec(memory_space=pltpu.HBM)
    weights = (ew, eb[None], dw, db, gw, gb[None], ow[None])
    scratch = [(pltpu.SMEM if w is db else vm)(w.shape, w.dtype) for w in weights] + scratch
    out = pl.pallas_call(
        functools.partial(kernel, n_t, n_l, D, L, C, S),
        out_shape=jax.ShapeDtypeStruct((D, L, N), F32),
        in_specs=[whole] * 11,
        out_specs=v,
        scratch_shapes=scratch,
        compiler_params=pltpu.CompilerParams(
            collective_id=0, has_side_effects=True, vmem_limit_bytes=67040000
        ),
        name="solver",
    )(x[0], y[0], m[0], land, *weights)
    return out[None]


def solution(mesh):
    tile = P(None, "tm", "lon", None)
    run = functools.partial(body, mesh.shape["tm"], mesh.shape["lon"])
    return jax.shard_map(
        run, mesh=mesh, in_specs=(tile, tile, tile, P("lon", None)) + (P(),) * 7,
        out_specs=tile, check_vma=False,
    )
```
